32 devices in a mesh: ice: 2 (over core), lat: 4 (over y, x), lon: 4 (over z).
Axes of the slice: x: 2, y: 2, z: 4, core: 2. Of those that a mesh axis runs over, the one named last changes fastest.
Arguments:
- adjoint_final: float32 [2, 4, 24, 128, 512], P('ice', None, None, 'lat', 'lon'), may hold values from -6 to 6
- land_mask: int32 [128, 512], P('lat', 'lon'), may hold values 0 or 1
- coupling_depth: int32 [2, 128, 512], P('ice', 'lat', 'lon'), may hold values from 1 to 24
- coupling_weight: float32 [2, 4, 128, 512], P('ice', None, 'lat', 'lon'), may hold values from 0.2 to 0.8
- diffusion: float32 [2, 2, 24, 128, 512], P(None, 'ice', None, 'lat', 'lon'), may hold values from 0.02 to 0.12
- velocity: float32 [2, 2, 2, 24, 128, 512], P(None, 'ice', None, None, 'lat', 'lon'), may hold values from -0.15 to 0.15
- mixing: float32 [2, 2, 24, 128, 512], P(None, 'ice', None, 'lat', 'lon'), may hold values from 0.05 to 0.3
Outputs:
- adjoint_start: float32 [2, 4, 24, 128, 512], P('ice', None, None, 'lat', 'lon')
The draws below stay inside these ranges and needn't reach their ends.
All inputs are finite; a program needn't handle non-finite values. No bound on the sum of `land_mask` on one device may be relied on, other than what follows from the above.
Results may differ from the reference program's by a relative error of at most 0.00002.
Values sent between devices are 32-bit elements; how exact they have to be, the bound alone decides.
A program may use at most 128 MiB of HBM per device.

```python
import jax
import jax.numpy as jnp

KL = 24
STEPS = 2
FIELDS = 4
SECT = 2
NY = 128
NX = 512


def place_ends(values, stream_key, least, high):
    place = [jax.random.randint(jax.random.fold_in(stream_key, axis), (), 0, length) for axis, length in enumerate(values.shape)]
    main_axis = values.shape.index(max(values.shape))
    neighbour = place[:main_axis] + [(place[main_axis] + 1) % values.shape[main_axis]] + place[main_axis + 1:]
    return values.at[tuple(place)].set(least).at[tuple(neighbour)].set(high)


def block_levels(own_key, extent, pieces, least, top_value):
    loudness = 1.0
    for axis_at, parts in pieces:
        heights = jax.random.uniform(jax.random.fold_in(jax.random.fold_in(own_key, 6), axis_at), (parts,), jnp.float32, least / len(pieces), top_value / len(pieces))
        loudness = loudness * jnp.repeat(jnp.exp(heights), extent[axis_at] // parts).reshape((-1,) + (1,) * (len(extent) - 1 - axis_at))
    return loudness


def gaussian(own_key, dims, deviation, most, shards=(), kind=jnp.bfloat16):
    values = jax.random.normal(own_key, dims, jnp.float32) * deviation
    if len(shards) > 0:
        values = block_levels(own_key, dims, shards, -0.22, 0.18) * values
    return jnp.clip(values, min=-most, max=most).astype(kind)


def setup_inputs(seed: int = 0) -> dict:
    keys = jax.random.split(jax.random.key(seed), 8)
    adjoint_final = gaussian(keys[0], (SECT, FIELDS, KL, NY, NX), 1.0, 6.0, ((0, 2), (3, 4), (4, 4)), jnp.float32)
    land_mask = place_ends((jax.random.randint(keys[1], (NY, NX), 0, 8) < 7).astype(jnp.int32), jax.random.fold_in(keys[1], 1), 0, 1)
    coupling_depth = place_ends(jax.random.randint(keys[2], (SECT, NY, NX), 1, KL + 1), jax.random.fold_in(keys[2], 1), 1, KL).astype(jnp.int32)
    coupling_weight = jnp.clip(0.2 + 0.6 * jax.random.uniform(keys[3], (SECT, FIELDS, NY, NX), jnp.float32) ** block_levels(keys[3], (SECT, FIELDS, NY, NX), ((0, 2), (2, 4), (3, 4)), -0.2, 0.2), 0.2, 0.8)
    diffusion = jnp.clip(0.02 + 0.09999999776482582 * jax.random.uniform(keys[4], (STEPS, SECT, KL, NY, NX), jnp.float32) ** block_levels(keys[4], (STEPS, SECT, KL, NY, NX), ((1, 2), (3, 4), (4, 4)), -0.2, 0.2), 0.02, 0.12)
    velocity = jnp.clip(jax.random.uniform(keys[5], (STEPS, SECT, 2, KL, NY, NX), jnp.float32, -0.15, 0.15) * block_levels(keys[5], (STEPS, SECT, 2, KL, NY, NX), ((1, 2), (4, 4), (5, 4)), -0.4, 0.0), -0.15, 0.15)
    mixing = jnp.clip(0.05 + 0.25 * jax.random.uniform(keys[6], (STEPS, SECT, KL, NY, NX), jnp.float32) ** block_levels(keys[6], (STEPS, SECT, KL, NY, NX), ((1, 2), (3, 4), (4, 4)), -0.2, 0.2), 0.05, 0.3)
    return dict(adjoint_final=adjoint_final, land_mask=land_mask, coupling_depth=coupling_depth, coupling_weight=coupling_weight, diffusion=diffusion, velocity=velocity, mixing=mixing)


def transport(field, land_cells, spread, zonal, merid, vertical):
    fold_sign = jnp.array([1.0, 1.0, -1.0, -1.0], field.dtype)[:, None, None, None]
    east_cell = jnp.roll(field, -1, axis=3)
    west_cell = jnp.roll(field, 1, axis=3)
    north_cell = jnp.concatenate([field[:, :, 1:, :], fold_sign * field[:, :, -1:, ::-1]], axis=2)
    south_cell = jnp.concatenate([jnp.zeros_like(field[:, :, :1, :]), field[:, :, :-1, :]], axis=2)
    upper_cell = jnp.concatenate([jnp.zeros_like(field[:, :1]), field[:, :-1]], axis=1)
    lower_cell = jnp.concatenate([field[:, 1:], jnp.zeros_like(field[:, :1])], axis=1)
    result = (1.0 - 4.0 * spread) * field + spread * (east_cell + west_cell + north_cell + south_cell)
    result = result - zonal * (east_cell - west_cell) - merid * (north_cell - south_cell)
    result = result + vertical * (upper_cell + lower_cell - 2.0 * field)
    return land_cells * result

def reference(adjoint_final, land_mask, coupling_depth, coupling_weight, diffusion, velocity, mixing):
    land_cells = land_mask.astype(jnp.float32)
    levels = adjoint_final.shape[2]
    level_index = jnp.arange(levels, dtype=jnp.int32)[None, :, None, None]
    depth_cells = coupling_depth[:, None, :, :]
    profile = jnp.where(level_index < depth_cells, 1.0, 0.0).astype(jnp.float32) / depth_cells.astype(jnp.float32)

    def one_step(state, moment):
        moved = jnp.stack([transport(state[section], land_cells, diffusion[moment, section], velocity[moment, section, 0], velocity[moment, section, 1], mixing[moment, section]) for section in range(2)])
        surface = moved[:, :, 0]
        gained = coupling_weight * (surface[::-1] - surface)
        return moved + gained[:, :, None] * profile[:, None]

    def forward(state):
        for moment in range(STEPS):
            state = one_step(state, moment)
        return state
    _, pullback = jax.vjp(forward, jnp.zeros_like(adjoint_final))
    return pullback(adjoint_final)[0]
```

```python
import functools

import jax
import jax.numpy as jnp
from jax import lax
from jax.experimental import pallas as pl
from jax.experimental.pallas import tpu as pltpu
from jax.sharding import PartitionSpec as P

MESH = pl.DeviceIdType.MESH
COUPLE, COL_E, COL_W, ROW_N, ROW_S, TOP_E, TOP_W, TOP_N, TOP_S = range(9)


def reversed_lanes(x, lane):
    width = x.shape[-1]
    bit = 1
    while bit < width:
        up = pltpu.roll(x, width - bit, x.ndim - 1)
        down = pltpu.roll(x, bit, x.ndim - 1)
        x = jnp.where((lane & bit) == 0, up, down)
        bit *= 2
    return x


def kernel(
    lats, lons, adj_h, mask_h, depth_h, weight_h, diff_h, vel_h, mix_h, out_h,
    field_a, field_b, diff, vel, mix, mask_i, depth, weight, vert,
    share, flux, col_out, col_w, col_e, top_col_out, top_col_w, top_col_e,
    north_out, south_out, north_in, south_in,
    top_north_out, top_south_out, top_north_in, top_south_in,
    load_sem, store_sem, send_sem, recv_sem,
):
    fields, levels, rows, cols = field_a.shape
    steps = diff.shape[0]
    chunk = store_sem.shape[0]
    span = levels // chunk
    ice, lat, lon = lax.axis_index("ice"), lax.axis_index("lat"), lax.axis_index("lon")
    partner = (1 - ice, lat, lon)
    east = (ice, lat, lax.rem(lon + 1, lons))
    west = (ice, lat, lax.rem(lon + lons - 1, lons))
    north = (ice, lat + 1, lon)
    south = (ice, lat - 1, lon)
    mirror = (ice, lat, lons - 1 - lon)
    top, bottom = lat == lats - 1, lat == 0

    loads = [
        pltpu.make_async_copy(depth_h.at[0], depth, load_sem.at[0]),
        pltpu.make_async_copy(weight_h.at[0], weight, load_sem.at[1]),
        pltpu.make_async_copy(mask_h, mask_i, load_sem.at[2]),
    ]
    for c in range(chunk):
        part = pl.ds(c * span, span)
        loads.append(pltpu.make_async_copy(adj_h.at[0, :, part], field_a.at[:, part], load_sem.at[3 + c]))
    coeffs = []
    for moment in range(steps):
        base = 3 + chunk + 3 * moment
        coeffs.append([
            pltpu.make_async_copy(diff_h.at[moment, 0], diff.at[moment], load_sem.at[base]),
            pltpu.make_async_copy(vel_h.at[moment, 0], vel.at[moment], load_sem.at[base + 1]),
            pltpu.make_async_copy(mix_h.at[moment, 0], mix.at[moment], load_sem.at[base + 2]),
        ])
    for copy in loads:
        copy.start()
    for moment in reversed(range(steps)):
        for copy in coeffs[moment]:
            copy.start()

    barrier = pltpu.get_barrier_semaphore()
    for peer in (partner, east, west):
        pl.semaphore_signal(barrier, inc=1, device_id=peer, device_id_type=MESH)

    @pl.when(top)
    def _():
        pl.semaphore_signal(barrier, inc=1, device_id=mirror, device_id_type=MESH)

    @pl.when(jnp.logical_not(top))
    def _():
        pl.semaphore_signal(barrier, inc=1, device_id=north, device_id_type=MESH)

    @pl.when(jnp.logical_not(bottom))
    def _():
        pl.semaphore_signal(barrier, inc=1, device_id=south, device_id_type=MESH)

    lane = lax.broadcasted_iota(jnp.int32, (rows, cols), 1)
    row = lax.broadcasted_iota(jnp.int32, (rows, cols), 0)
    lane8 = lax.broadcasted_iota(jnp.int32, (8, cols), 1)
    row8 = lax.broadcasted_iota(jnp.int32, (8, cols), 0)
    ends8 = jnp.logical_or(lane8 == 0, lane8 == cols - 1)
    for q in range(fields):
        vert[q, 0] = jnp.zeros((rows, cols), jnp.float32)
        vert[q, levels + 1] = jnp.zeros((rows, cols), jnp.float32)

    @pl.when(bottom)
    def _():
        south_in[...] = jnp.zeros_like(south_in)
        top_south_in[...] = jnp.zeros_like(top_south_in)

    def remote(step, which, src, dst, peer):
        return pltpu.make_async_remote_copy(
            src_ref=src, dst_ref=dst, send_sem=send_sem.at[step, which],
            recv_sem=recv_sem.at[step, which], device_id=peer, device_id_type=MESH,
        )

    def row_copies(step, which_n, which_s, n_out, s_out, n_in, s_in):
        return [
            (remote(step, which_s, n_out.at[step], s_in.at[step], north), jnp.logical_not(top)),
            (remote(step, which_n, n_out.at[step], n_in.at[step], mirror), top),
            (remote(step, which_n, s_out.at[step], n_in.at[step], south), jnp.logical_not(bottom)),
        ]

    def start_rows(copies):
        for copy, go in copies:
            pl.when(go)(copy.start)

    half = fields // 2

    def edges(step, moment, k, src, packed, place, put_rows):
        mask = mask_i[...].astype(jnp.float32)
        d, z = diff[moment, k] * mask, vel[moment, 0, k] * mask
        v = mix[moment, k] * mask
        both = d + jnp.where(lane == cols - 1, -z, z)
        last, first = slice(rows - 1, rows), slice(0, 1)
        b_last, b_first = vel[moment, 1, k, last] * mask[last], vel[moment, 1, k, first] * mask[first]
        to_north, to_south = d[last] - b_last, d[first] + b_first
        packed = list(packed)
        for q in range(fields):
            a = src[q, k]
            vert[q, k + 1] = v * a
            slot, spot = place(q)
            turned = pltpu.roll(both * a, 2 * spot + 1, 1)
            packed[slot] = jnp.where((lane >> 1) == spot, turned, packed[slot])
            put_rows(q, to_north * a[last], to_south * a[first])
        return tuple(packed)

    def interior(moment, k, src, dst):
        mask = mask_i[...].astype(jnp.float32)
        d, z, b = diff[moment, k] * mask, vel[moment, 0, k] * mask, vel[moment, 1, k] * mask
        own = mask - 4.0 * d - 2.0 * (mix[moment, k] * mask)
        eastward = jnp.where(lane == cols - 1, 0.0, d - z)
        westward = jnp.where(lane == 0, 0.0, d + z)
        northward = jnp.where(row == rows - 1, 0.0, d - b)
        southward = jnp.where(row == 0, 0.0, d + b)
        for q in range(fields):
            a = src[q, k]
            total = own * a + vert[q, k] + vert[q, k + 2]
            total = total + pltpu.roll(eastward * a, 1, 1) + pltpu.roll(westward * a, cols - 1, 1)
            total = total + pltpu.roll(northward * a, 1, 0) + pltpu.roll(southward * a, rows - 1, 0)
            dst[q, k] = total

    def finish(k, q, dst, packed, spot, from_south, from_north):
        parts = []
        for r in range(0, rows, 8):
            turned = pltpu.roll(packed[r:r + 8], cols - 1 - 2 * spot, 1)
            total = dst[q, k, r:r + 8] + jnp.where(ends8, turned, 0.0)
            if r == 0:
                total = total + jnp.where(row8 == 0, from_south, 0.0)
            if r == rows - 8:
                total = total + jnp.where(row8 == 7, from_north, 0.0)
            dst[q, k, r:r + 8] = total
            parts.append(total)
        return jnp.concatenate(parts, axis=0)

    def joined(from_west, from_east):
        return jnp.where(
            (lane & 1) == 1, pltpu.roll(from_west, 1, 1), pltpu.roll(from_east, cols - 1, 1)
        )

    loads[0].wait()
    zero = jnp.zeros((rows, cols), jnp.float32)
    sums = (zero,) * fields
    for c in range(chunk):
        loads[3 + c].wait()

        def add(k, sums):
            live = k < depth[...]
            return tuple(s + jnp.where(live, field_a[q, k], 0.0) for q, s in enumerate(sums))

        sums = lax.fori_loop(c * span, (c + 1) * span, add, sums)
    loads[1].wait()
    loads[2].wait()

    @pl.when(bottom)
    def _():
        pl.semaphore_wait(barrier, 4)

    @pl.when(jnp.logical_not(bottom))
    def _():
        pl.semaphore_wait(barrier, 5)

    pending = []
    stores = []
    for step in range(steps):
        moment = steps - 1 - step
        src, dst = (field_a, field_b) if step % 2 == 0 else (field_b, field_a)
        final = step == steps - 1
        scale = 1.0 / depth[...].astype(jnp.float32)
        for q in range(fields):
            share[step, q] = weight[q] * (scale * sums[q])
        couple = remote(step, COUPLE, share.at[step], flux.at[step], partner)
        couple.start()
        for copy in coeffs[moment]:
            copy.wait()

        for q in range(fields):
            north_out[step, q, 0:1] = jnp.zeros((1, cols), jnp.float32)
            south_out[step, q, 0:1] = jnp.zeros((1, cols), jnp.float32)

        def deep(k, packed):
            def put(q, up, down):
                north_out[step, q, pl.ds(k, 1)] = up
                south_out[step, q, pl.ds(k, 1)] = down

            return edges(
                step, moment, k, src, packed, lambda q: (q // half, (q % half) * levels + k), put
            )

        packed = lax.fori_loop(1, levels, deep, (zero, zero))
        for slot in range(2):
            col_out[step, slot] = packed[slot]
        send_e = remote(step, COL_E, col_out.at[step], col_w.at[step], east)
        send_w = remote(step, COL_W, col_out.at[step], col_e.at[step], west)
        send_rows = row_copies(step, ROW_N, ROW_S, north_out, south_out, north_in, south_in)
        start_rows(send_rows)
        send_e.start()
        send_w.start()

        couple.wait_recv()
        for q in range(fields):
            src[q, 0] = src[q, 0] + (flux[step, q] - share[step, q])

        def put_top(q, up, down):
            top_north_out[step, q:q + 1] = up
            top_south_out[step, q:q + 1] = down

        (top_packed,) = edges(step, moment, 0, src, (zero,), lambda q: (0, q), put_top)
        top_col_out[step] = top_packed
        top_e = remote(step, TOP_E, top_col_out.at[step], top_col_w.at[step], east)
        top_w = remote(step, TOP_W, top_col_out.at[step], top_col_e.at[step], west)
        top_rows = row_copies(
            step, TOP_N, TOP_S, top_north_out, top_south_out, top_north_in, top_south_in
        )
        start_rows(top_rows)
        top_e.start()
        top_w.start()

        def inner(k, carry):
            interior(moment, k, src, dst)
            return carry

        lax.fori_loop(0, levels, inner, 0)

        for copy in (send_e, send_w, top_e, top_w):
            copy.wait_recv()
        for copies in (send_rows, top_rows):
            copies[1][0].wait_recv()
            pl.when(jnp.logical_not(bottom))(copies[0][0].wait_recv)

        @pl.when(top)
        def _():
            lane_s = lax.broadcasted_iota(jnp.int32, (levels, cols), 1)
            for q in range(fields):
                turned = reversed_lanes(north_in[step, q], lane_s)
                north_in[step, q] = turned if q < half else -turned
            lane_f = lax.broadcasted_iota(jnp.int32, (fields, cols), 1)
            sign = lax.broadcasted_iota(jnp.int32, (fields, cols), 0)
            turned = reversed_lanes(top_north_in[step], lane_f)
            top_north_in[step] = jnp.where(sign < half, turned, -turned)

        pair = [joined(col_w[step, slot], col_e[step, slot]) for slot in range(2)]
        top_pair = joined(top_col_w[step], top_col_e[step])
        sums = []
        for q in range(fields):
            total = finish(
                0, q, dst, top_pair, q,
                top_south_in[step, q:q + 1], top_north_in[step, q:q + 1],
            )
            sums.append(total)
        sums = tuple(sums)
        for c in range(chunk):

            def last(k, sums):
                out = []
                for q in range(fields):
                    total = finish(
                        k, q, dst, pair[q // half], (q % half) * levels + k,
                        south_in[step, q, pl.ds(k, 1)], north_in[step, q, pl.ds(k, 1)],
                    )
                    if not final:
                        out.append(sums[q] + jnp.where(k < depth[...], total, 0.0))
                return tuple(out) if not final else sums

            lower = max(1, c * span)
            sums = lax.fori_loop(lower, (c + 1) * span, last, sums if not final else 0)
            if final:
                part = pl.ds(c * span, span)
                copy = pltpu.make_async_copy(dst.at[:, part], out_h.at[0, :, part], store_sem.at[c])
                copy.start()
                stores.append(copy)

        pending += [(couple, None), (send_e, None), (send_w, None), (top_e, None), (top_w, None)]
        pending += send_rows + top_rows

    for copy, go in pending:
        if go is None:
            copy.wait_send()
        else:
            pl.when(go)(copy.wait_send)
    for copy in stores:
        copy.wait()


def solution(mesh):
    lats, lons = mesh.shape["lat"], mesh.shape["lon"]

    def shards(adjoint, land_mask, coupling_depth, coupling_weight, diffusion, velocity, mixing):
        _, fields, levels, rows, cols = adjoint.shape
        steps = diffusion.shape[0]
        chunk = 3
        f32 = jnp.float32
        block = (rows, cols)
        column = pltpu.VMEM((steps, 2, rows, cols), f32)
        top_column = pltpu.VMEM((steps, rows, cols), f32)
        edge = pltpu.VMEM((steps, fields, levels, cols), f32)
        top_edge = pltpu.VMEM((steps, fields, cols), f32)
        return pl.pallas_call(
            functools.partial(kernel, lats, lons),
            out_shape=jax.ShapeDtypeStruct(adjoint.shape, f32),
            in_specs=[pl.BlockSpec(memory_space=pl.ANY)] * 7,
            out_specs=pl.BlockSpec(memory_space=pl.ANY),
            scratch_shapes=[
                pltpu.VMEM((fields, levels, rows, cols), f32),
                pltpu.VMEM((fields, levels, rows, cols), f32),
                pltpu.VMEM((steps, levels, rows, cols), f32),
                pltpu.VMEM((steps, 2, levels, rows, cols), f32),
                pltpu.VMEM((steps, levels, rows, cols), f32),
                pltpu.VMEM(block, jnp.int32),
                pltpu.VMEM(block, jnp.int32),
                pltpu.VMEM((fields, rows, cols), f32),
                pltpu.VMEM((fields, levels + 2, rows, cols), f32),
                pltpu.VMEM((steps, fields, rows, cols), f32),
                pltpu.VMEM((steps, fields, rows, cols), f32),
                column, column, column,
                top_column, top_column, top_column,
                edge, edge, edge, edge,
                top_edge, top_edge, top_edge, top_edge,
                pltpu.SemaphoreType.DMA((3 + chunk + 3 * steps,)),
                pltpu.SemaphoreType.DMA((chunk,)),
                pltpu.SemaphoreType.DMA((steps, 12)),
                pltpu.SemaphoreType.DMA((steps, 9)),
            ],
            compiler_params=pltpu.CompilerParams(
                collective_id=0, has_side_effects=True, vmem_limit_bytes=60 * 1024 * 1024
            ),
            name="adjoint",
        )(adjoint, land_mask, coupling_depth, coupling_weight, diffusion, velocity, mixing)

    in_specs = (
        P("ice", None, None, "lat", "lon"),
        P("lat", "lon"),
        P("ice", "lat", "lon"),
        P("ice", None, "lat", "lon"),
        P(None, "ice", None, "lat", "lon"),
        P(None, "ice", None, None, "lat", "lon"),
        P(None, "ice", None, "lat", "lon"),
    )
    out_specs = P("ice", None, None, "lat", "lon")
    return jax.shard_map(shards, mesh=mesh, in_specs=in_specs, out_specs=out_specs, check_vma=False)
```

```python
import functools

import jax
import jax.numpy as jnp
from jax import lax
from jax.experimental import pallas as pl
from jax.experimental.pallas import tpu as pltpu
from jax.sharding import PartitionSpec as P

MESH = pl.DeviceIdType.MESH
EDGE, INNER, LAST = 8, 4, 8
COUPLE, COL_E, COL_W, ROW_N, ROW_S, TOP_E, TOP_W, TOP_N, TOP_S = range(9)


def levels_loop(lower, upper, body, carry, times):
    whole = (upper - lower) // times

    def some(i, carry):
        for j in range(times):
            carry = body(lower + i * times + j, carry)
        return carry

    if whole > 0:
        carry = lax.fori_loop(0, whole, some, carry)
    for k in range(lower + whole * times, upper):
        carry = body(k, carry)
    return carry


def reversed_lanes(x, lane):
    width = x.shape[-1]
    bit = 1
    while bit < width:
        up = pltpu.roll(x, width - bit, x.ndim - 1)
        down = pltpu.roll(x, bit, x.ndim - 1)
        x = jnp.where((lane & bit) == 0, up, down)
        bit *= 2
    return x


def kernel(
    lats, lons, adj_h, mask_h, depth_h, weight_h, diff_h, vel_h, mix_h, out_h,
    field_a, field_b, diff, vel, mix, mask_i, depth, weight, vert,
    share, flux, col_out, col_w, col_e, top_col_out, top_col_w, top_col_e,
    north_out, south_out, north_in, south_in,
    top_north_out, top_south_out, top_north_in, top_south_in,
    load_sem, store_sem, send_sem, recv_sem,
):
    fields, levels, rows, cols = field_a.shape
    steps = diff.shape[0]
    chunk = store_sem.shape[0]
    span = levels // chunk
    ice, lat, lon = lax.axis_index("ice"), lax.axis_index("lat"), lax.axis_index("lon")
    partner = (1 - ice, lat, lon)
    east = (ice, lat, lax.rem(lon + 1, lons))
    west = (ice, lat, lax.rem(lon + lons - 1, lons))
    north = (ice, lat + 1, lon)
    south = (ice, lat - 1, lon)
    mirror = (ice, lat, lons - 1 - lon)
    top, bottom = lat == lats - 1, lat == 0

    loads = [
        pltpu.make_async_copy(depth_h.at[0], depth, load_sem.at[0]),
        pltpu.make_async_copy(weight_h.at[0], weight, load_sem.at[1]),
        pltpu.make_async_copy(mask_h, mask_i, load_sem.at[2]),
    ]
    for c in range(chunk):
        part = pl.ds(c * span, span)
        loads.append(pltpu.make_async_copy(adj_h.at[0, :, part], field_a.at[:, part], load_sem.at[3 + c]))
    coeffs = []
    for moment in range(steps):
        base = 3 + chunk + 3 * moment
        coeffs.append([
            pltpu.make_async_copy(diff_h.at[moment, 0], diff.at[moment], load_sem.at[base]),
            pltpu.make_async_copy(vel_h.at[moment, 0], vel.at[moment], load_sem.at[base + 1]),
            pltpu.make_async_copy(mix_h.at[moment, 0], mix.at[moment], load_sem.at[base + 2]),
        ])
    for copy in loads:
        copy.start()
    for moment in reversed(range(steps)):
        for copy in coeffs[moment]:
            copy.start()

    barrier = pltpu.get_barrier_semaphore()
    for peer in (partner, east, west):
        pl.semaphore_signal(barrier, inc=1, device_id=peer, device_id_type=MESH)

    @pl.when(top)
    def _():
        pl.semaphore_signal(barrier, inc=1, device_id=mirror, device_id_type=MESH)

    @pl.when(jnp.logical_not(top))
    def _():
        pl.semaphore_signal(barrier, inc=1, device_id=north, device_id_type=MESH)

    @pl.when(jnp.logical_not(bottom))
    def _():
        pl.semaphore_signal(barrier, inc=1, device_id=south, device_id_type=MESH)

    lane = lax.broadcasted_iota(jnp.int32, (rows, cols), 1)
    row = lax.broadcasted_iota(jnp.int32, (rows, cols), 0)
    lane8 = lax.broadcasted_iota(jnp.int32, (8, cols), 1)
    row8 = lax.broadcasted_iota(jnp.int32, (8, cols), 0)
    ends8 = jnp.logical_or(lane8 == 0, lane8 == cols - 1)
    for q in range(fields):
        vert[q, 0] = jnp.zeros((rows, cols), jnp.float32)
        vert[q, levels + 1] = jnp.zeros((rows, cols), jnp.float32)

    @pl.when(bottom)
    def _():
        south_in[...] = jnp.zeros_like(south_in)
        top_south_in[...] = jnp.zeros_like(top_south_in)

    def remote(step, which, src, dst, peer):
        return pltpu.make_async_remote_copy(
            src_ref=src, dst_ref=dst, send_sem=send_sem.at[step, which],
            recv_sem=recv_sem.at[step, which], device_id=peer, device_id_type=MESH,
        )

    def row_copies(step, which_n, which_s, n_out, s_out, n_in, s_in):
        return [
            (remote(step, which_s, n_out.at[step], s_in.at[step], north), jnp.logical_not(top)),
            (remote(step, which_n, n_out.at[step], n_in.at[step], mirror), top),
            (remote(step, which_n, s_out.at[step], n_in.at[step], south), jnp.logical_not(bottom)),
        ]

    def start_rows(copies):
        for copy, go in copies:
            pl.when(go)(copy.start)

    half = fields // 2

    def edges(step, moment, k, src, packed, place, put_rows):
        mask = mask_i[...].astype(jnp.float32)
        d, z = diff[moment, k] * mask, vel[moment, 0, k] * mask
        v = mix[moment, k] * mask
        both = d + jnp.where(lane == cols - 1, -z, z)
        last, first = slice(rows - 1, rows), slice(0, 1)
        b_last, b_first = vel[moment, 1, k, last] * mask[last], vel[moment, 1, k, first] * mask[first]
        to_north, to_south = d[last] - b_last, d[first] + b_first
        packed = list(packed)
        for q in range(fields):
            a = src[q, k]
            vert[q, k + 1] = v * a
            slot, spot = place(q)
            turned = pltpu.roll(both * a, 2 * spot + 1, 1)
            packed[slot] = jnp.where((lane >> 1) == spot, turned, packed[slot])
            put_rows(q, to_north * a[last], to_south * a[first])
        return tuple(packed)

    def interior(moment, k, src, dst):
        mask = mask_i[...].astype(jnp.float32)
        d, z, b = diff[moment, k] * mask, vel[moment, 0, k] * mask, vel[moment, 1, k] * mask
        own = mask - 4.0 * d - 2.0 * (mix[moment, k] * mask)
        eastward = jnp.where(lane == cols - 1, 0.0, d - z)
        westward = jnp.where(lane == 0, 0.0, d + z)
        northward = jnp.where(row == rows - 1, 0.0, d - b)
        southward = jnp.where(row == 0, 0.0, d + b)
        for q in range(fields):
            a = src[q, k]
            total = own * a + vert[q, k] + vert[q, k + 2]
            total = total + pltpu.roll(eastward * a, 1, 1) + pltpu.roll(westward * a, cols - 1, 1)
            total = total + pltpu.roll(northward * a, 1, 0) + pltpu.roll(southward * a, rows - 1, 0)
            dst[q, k] = total

    def finish(k, q, dst, packed, spot, from_south, from_north):
        parts = []
        for r in range(0, rows, 8):
            turned = pltpu.roll(packed[r:r + 8], cols - 1 - 2 * spot, 1)
            total = dst[q, k, r:r + 8] + jnp.where(ends8, turned, 0.0)
            if r == 0:
                total = total + jnp.where(row8 == 0, from_south, 0.0)
            if r == rows - 8:
                total = total + jnp.where(row8 == 7, from_north, 0.0)
            dst[q, k, r:r + 8] = total
            parts.append(total)
        return jnp.concatenate(parts, axis=0)

    def joined(from_west, from_east):
        return jnp.where(
            (lane & 1) == 1, pltpu.roll(from_west, 1, 1), pltpu.roll(from_east, cols - 1, 1)
        )

    loads[0].wait()
    zero = jnp.zeros((rows, cols), jnp.float32)
    sums = (zero,) * fields
    for c in range(chunk):
        loads[3 + c].wait()

        def add(k, sums):
            live = k < depth[...]
            return tuple(s + jnp.where(live, field_a[q, k], 0.0) for q, s in enumerate(sums))

        sums = levels_loop(c * span, (c + 1) * span, add, sums, 4)
    loads[1].wait()
    loads[2].wait()

    @pl.when(bottom)
    def _():
        pl.semaphore_wait(barrier, 4)

    @pl.when(jnp.logical_not(bottom))
    def _():
        pl.semaphore_wait(barrier, 5)

    pending = []
    stores = []
    for step in range(steps):
        moment = steps - 1 - step
        src, dst = (field_a, field_b) if step % 2 == 0 else (field_b, field_a)
        final = step == steps - 1
        scale = 1.0 / depth[...].astype(jnp.float32)
        for q in range(fields):
            share[step, q] = weight[q] * (scale * sums[q])
        couple = remote(step, COUPLE, share.at[step], flux.at[step], partner)
        couple.start()
        for copy in coeffs[moment]:
            copy.wait()

        for q in range(fields):
            north_out[step, q, 0:1] = jnp.zeros((1, cols), jnp.float32)
            south_out[step, q, 0:1] = jnp.zeros((1, cols), jnp.float32)

        def deep(k, packed):
            def put(q, up, down):
                north_out[step, q, pl.ds(k, 1)] = up
                south_out[step, q, pl.ds(k, 1)] = down

            return edges(
                step, moment, k, src, packed, lambda q: (q // half, (q % half) * levels + k), put
            )

        packed = levels_loop(1, levels, deep, (zero, zero), EDGE)
        for slot in range(2):
            col_out[step, slot] = packed[slot]
        send_e = remote(step, COL_E, col_out.at[step], col_w.at[step], east)
        send_w = remote(step, COL_W, col_out.at[step], col_e.at[step], west)
        send_rows = row_copies(step, ROW_N, ROW_S, north_out, south_out, north_in, south_in)
        start_rows(send_rows)
        send_e.start()
        send_w.start()

        couple.wait_recv()
        for q in range(fields):
            src[q, 0] = src[q, 0] + (flux[step, q] - share[step, q])

        def put_top(q, up, down):
            top_north_out[step, q:q + 1] = up
            top_south_out[step, q:q + 1] = down

        (top_packed,) = edges(step, moment, 0, src, (zero,), lambda q: (0, q), put_top)
        top_col_out[step] = top_packed
        top_e = remote(step, TOP_E, top_col_out.at[step], top_col_w.at[step], east)
        top_w = remote(step, TOP_W, top_col_out.at[step], top_col_e.at[step], west)
        top_rows = row_copies(
            step, TOP_N, TOP_S, top_north_out, top_south_out, top_north_in, top_south_in
        )
        start_rows(top_rows)
        top_e.start()
        top_w.start()

        def inner(k, carry):
            interior(moment, k, src, dst)
            return carry

        levels_loop(0, levels, inner, 0, INNER)

        for copy in (send_e, send_w, top_e, top_w):
            copy.wait_recv()
        for copies in (send_rows, top_rows):
            copies[1][0].wait_recv()
            pl.when(jnp.logical_not(bottom))(copies[0][0].wait_recv)

        @pl.when(top)
        def _():
            lane_s = lax.broadcasted_iota(jnp.int32, (levels, cols), 1)
            for q in range(fields):
                turned = reversed_lanes(north_in[step, q], lane_s)
                north_in[step, q] = turned if q < half else -turned
            lane_f = lax.broadcasted_iota(jnp.int32, (fields, cols), 1)
            sign = lax.broadcasted_iota(jnp.int32, (fields, cols), 0)
            turned = reversed_lanes(top_north_in[step], lane_f)
            top_north_in[step] = jnp.where(sign < half, turned, -turned)

        pair = [joined(col_w[step, slot], col_e[step, slot]) for slot in range(2)]
        top_pair = joined(top_col_w[step], top_col_e[step])
        sums = []
        for q in range(fields):
            total = finish(
                0, q, dst, top_pair, q,
                top_south_in[step, q:q + 1], top_north_in[step, q:q + 1],
            )
            sums.append(total)
        sums = tuple(sums)
        for c in range(chunk):

            def last(k, sums):
                out = []
                for q in range(fields):
                    total = finish(
                        k, q, dst, pair[q // half], (q % half) * levels + k,
                        south_in[step, q, pl.ds(k, 1)], north_in[step, q, pl.ds(k, 1)],
                    )
                    if not final:
                        out.append(sums[q] + jnp.where(k < depth[...], total, 0.0))
                return tuple(out) if not final else sums

            lower = max(1, c * span)
            sums = levels_loop(lower, (c + 1) * span, last, sums if not final else 0, LAST)
            if final:
                part = pl.ds(c * span, span)
                copy = pltpu.make_async_copy(dst.at[:, part], out_h.at[0, :, part], store_sem.at[c])
                copy.start()
                stores.append(copy)

        pending += [(couple, None), (send_e, None), (send_w, None), (top_e, None), (top_w, None)]
        pending += send_rows + top_rows

    for copy, go in pending:
        if go is None:
            copy.wait_send()
        else:
            pl.when(go)(copy.wait_send)
    for copy in stores:
        copy.wait()


def solution(mesh):
    lats, lons = mesh.shape["lat"], mesh.shape["lon"]

    def shards(adjoint, land_mask, coupling_depth, coupling_weight, diffusion, velocity, mixing):
        _, fields, levels, rows, cols = adjoint.shape
        steps = diffusion.shape[0]
        chunk = 3
        f32 = jnp.float32
        block = (rows, cols)
        column = pltpu.VMEM((steps, 2, rows, cols), f32)
        top_column = pltpu.VMEM((steps, rows, cols), f32)
        edge = pltpu.VMEM((steps, fields, levels, cols), f32)
        top_edge = pltpu.VMEM((steps, fields, cols), f32)
        return pl.pallas_call(
            functools.partial(kernel, lats, lons),
            out_shape=jax.ShapeDtypeStruct(adjoint.shape, f32),
            in_specs=[pl.BlockSpec(memory_space=pl.ANY)] * 7,
            out_specs=pl.BlockSpec(memory_space=pl.ANY),
            scratch_shapes=[
                pltpu.VMEM((fields, levels, rows, cols), f32),
                pltpu.VMEM((fields, levels, rows, cols), f32),
                pltpu.VMEM((steps, levels, rows, cols), f32),
                pltpu.VMEM((steps, 2, levels, rows, cols), f32),
                pltpu.VMEM((steps, levels, rows, cols), f32),
                pltpu.VMEM(block, jnp.int32),
                pltpu.VMEM(block, jnp.int32),
                pltpu.VMEM((fields, rows, cols), f32),
                pltpu.VMEM((fields, levels + 2, rows, cols), f32),
                pltpu.VMEM((steps, fields, rows, cols), f32),
                pltpu.VMEM((steps, fields, rows, cols), f32),
                column, column, column,
                top_column, top_column, top_column,
                edge, edge, edge, edge,
                top_edge, top_edge, top_edge, top_edge,
                pltpu.SemaphoreType.DMA((3 + chunk + 3 * steps,)),
                pltpu.SemaphoreType.DMA((chunk,)),
                pltpu.SemaphoreType.DMA((steps, 12)),
                pltpu.SemaphoreType.DMA((steps, 9)),
            ],
            compiler_params=pltpu.CompilerParams(
                collective_id=0, has_side_effects=True, vmem_limit_bytes=60 * 1024 * 1024
            ),
            name="adjoint",
        )(adjoint, land_mask, coupling_depth, coupling_weight, diffusion, velocity, mixing)

    in_specs = (
        P("ice", None, None, "lat", "lon"),
        P("lat", "lon"),
        P("ice", "lat", "lon"),
        P("ice", None, "lat", "lon"),
        P(None, "ice", None, "lat", "lon"),
        P(None, "ice", None, None, "lat", "lon"),
        P(None, "ice", None, "lat", "lon"),
    )
    out_specs = P("ice", None, None, "lat", "lon")
    return jax.shard_map(shards, mesh=mesh, in_specs=in_specs, out_specs=out_specs, check_vma=False)
```

```python
import functools

import jax
import jax.numpy as jnp
from jax import lax
from jax.experimental import pallas as pl
from jax.experimental.pallas import tpu as pltpu
from jax.sharding import PartitionSpec as P

MESH = pl.DeviceIdType.MESH
EDGE, INNER, LAST = 8, 4, 8
COUPLE, COL_E, COL_W, ROW_N, ROW_S, TOP_E, TOP_W, TOP_N, TOP_S = range(9)


def levels_loop(lower, upper, body, carry, times):
    whole = (upper - lower) // times

    def some(i, carry):
        for j in range(times):
            carry = body(lower + i * times + j, carry)
        return carry

    if whole > 0:
        carry = lax.fori_loop(0, whole, some, carry)
    for k in range(lower + whole * times, upper):
        carry = body(k, carry)
    return carry


def reversed_lanes(x, lane):
    width = x.shape[-1]
    bit = 1
    while bit < width:
        up = pltpu.roll(x, width - bit, x.ndim - 1)
        down = pltpu.roll(x, bit, x.ndim - 1)
        x = jnp.where((lane & bit) == 0, up, down)
        bit *= 2
    return x


def kernel(
    lats, lons, adj_h, mask_h, depth_h, weight_h, diff_h, vel_h, mix_h, out_h,
    field_a, field_b, diff, vel, mix, mask_i, depth, weight, vert,
    share, flux, col_out, col_w, col_e, top_col_out, top_col_w, top_col_e,
    north_out, south_out, north_in, south_in,
    top_north_out, top_south_out, top_north_in, top_south_in,
    load_sem, store_sem, send_sem, recv_sem,
):
    fields, levels, rows, cols = field_a.shape
    steps = diff.shape[0]
    chunk = store_sem.shape[0]
    span = levels // chunk
    ice, lat, lon = lax.axis_index("ice"), lax.axis_index("lat"), lax.axis_index("lon")
    partner = (1 - ice, lat, lon)
    east = (ice, lat, lax.rem(lon + 1, lons))
    west = (ice, lat, lax.rem(lon + lons - 1, lons))
    north = (ice, lat + 1, lon)
    south = (ice, lat - 1, lon)
    mirror = (ice, lat, lons - 1 - lon)
    top, bottom = lat == lats - 1, lat == 0

    loads = [
        pltpu.make_async_copy(depth_h.at[0], depth, load_sem.at[0]),
        pltpu.make_async_copy(weight_h.at[0], weight, load_sem.at[1]),
        pltpu.make_async_copy(mask_h, mask_i, load_sem.at[2]),
    ]
    for c in range(chunk):
        part = pl.ds(c * span, span)
        loads.append(pltpu.make_async_copy(adj_h.at[0, :, part], field_a.at[:, part], load_sem.at[3 + c]))
    coeffs = []
    for moment in range(steps):
        base = 3 + chunk + 3 * moment
        coeffs.append([
            pltpu.make_async_copy(diff_h.at[moment, 0], diff.at[moment], load_sem.at[base]),
            pltpu.make_async_copy(vel_h.at[moment, 0], vel.at[moment], load_sem.at[base + 1]),
            pltpu.make_async_copy(mix_h.at[moment, 0], mix.at[moment], load_sem.at[base + 2]),
        ])
    for copy in loads:
        copy.start()
    for moment in reversed(range(steps)):
        for copy in coeffs[moment]:
            copy.start()

    barrier = pltpu.get_barrier_semaphore()
    for peer in (partner, east, west):
        pl.semaphore_signal(barrier, inc=1, device_id=peer, device_id_type=MESH)

    @pl.when(top)
    def _():
        pl.semaphore_signal(barrier, inc=1, device_id=mirror, device_id_type=MESH)

    @pl.when(jnp.logical_not(top))
    def _():
        pl.semaphore_signal(barrier, inc=1, device_id=north, device_id_type=MESH)

    @pl.when(jnp.logical_not(bottom))
    def _():
        pl.semaphore_signal(barrier, inc=1, device_id=south, device_id_type=MESH)

    lane = lax.broadcasted_iota(jnp.int32, (rows, cols), 1)
    row = lax.broadcasted_iota(jnp.int32, (rows, cols), 0)
    lane8 = lax.broadcasted_iota(jnp.int32, (8, cols), 1)
    row8 = lax.broadcasted_iota(jnp.int32, (8, cols), 0)
    ends8 = jnp.logical_or(lane8 == 0, lane8 == cols - 1)
    for q in range(fields):
        vert[q, 0] = jnp.zeros((rows, cols), jnp.float32)
        vert[q, levels + 1] = jnp.zeros((rows, cols), jnp.float32)

    @pl.when(bottom)
    def _():
        south_in[...] = jnp.zeros_like(south_in)
        top_south_in[...] = jnp.zeros_like(top_south_in)

    def remote(step, which, src, dst, peer):
        return pltpu.make_async_remote_copy(
            src_ref=src, dst_ref=dst, send_sem=send_sem.at[step, which],
            recv_sem=recv_sem.at[step, which], device_id=peer, device_id_type=MESH,
        )

    def row_copies(step, which_n, which_s, n_out, s_out, n_in, s_in):
        return [
            (remote(step, which_s, n_out.at[step], s_in.at[step], north), jnp.logical_not(top)),
            (remote(step, which_n, n_out.at[step], n_in.at[step], mirror), top),
            (remote(step, which_n, s_out.at[step], n_in.at[step], south), jnp.logical_not(bottom)),
        ]

    def start_rows(copies):
        for copy, go in copies:
            pl.when(go)(copy.start)

    half = fields // 2

    def edges(step, moment, k, src, packed, place, put_rows):
        mask = mask_i[...].astype(jnp.float32)
        d, z = diff[moment, k] * mask, vel[moment, 0, k] * mask
        v = mix[moment, k] * mask
        both = d + jnp.where(lane == cols - 1, -z, z)
        last, first = slice(rows - 1, rows), slice(0, 1)
        b_last, b_first = vel[moment, 1, k, last] * mask[last], vel[moment, 1, k, first] * mask[first]
        to_north, to_south = d[last] - b_last, d[first] + b_first
        packed = list(packed)
        for q in range(fields):
            a = src[q, k]
            vert[q, k + 1] = v * a
            slot, spot = place(q)
            turned = pltpu.roll(both * a, 2 * spot + 1, 1)
            packed[slot] = jnp.where((lane >> 1) == spot, turned, packed[slot])
            put_rows(q, to_north * a[last], to_south * a[first])
        return tuple(packed)

    def interior(moment, k, src, dst):
        mask = mask_i[...].astype(jnp.float32)
        d, z, b = diff[moment, k] * mask, vel[moment, 0, k] * mask, vel[moment, 1, k] * mask
        own = mask - 4.0 * d - 2.0 * (mix[moment, k] * mask)
        eastward = jnp.where(lane == cols - 1, 0.0, d - z)
        westward = jnp.where(lane == 0, 0.0, d + z)
        northward = jnp.where(row == rows - 1, 0.0, d - b)
        southward = jnp.where(row == 0, 0.0, d + b)
        for q in range(fields):
            a = src[q, k]
            total = own * a + vert[q, k] + vert[q, k + 2]
            total = total + pltpu.roll(eastward * a, 1, 1) + pltpu.roll(westward * a, cols - 1, 1)
            total = total + pltpu.roll(northward * a, 1, 0) + pltpu.roll(southward * a, rows - 1, 0)
            dst[q, k] = total

    def finish(k, q, dst, packed, spot, from_south, from_north):
        parts = []
        for r in range(0, rows, 8):
            turned = pltpu.roll(packed[r:r + 8], cols - 1 - 2 * spot, 1)
            total = dst[q, k, r:r + 8] + jnp.where(ends8, turned, 0.0)
            if r == 0:
                total = total + jnp.where(row8 == 0, from_south, 0.0)
            if r == rows - 8:
                total = total + jnp.where(row8 == 7, from_north, 0.0)
            dst[q, k, r:r + 8] = total
            parts.append(total)
        return jnp.concatenate(parts, axis=0)

    def joined(from_west, from_east):
        return jnp.where(
            (lane & 1) == 1, pltpu.roll(from_west, 1, 1), pltpu.roll(from_east, cols - 1, 1)
        )

    loads[0].wait()
    zero = jnp.zeros((rows, cols), jnp.float32)
    sums = (zero,) * fields
    for c in range(chunk):
        loads[3 + c].wait()

        def add(k, sums):
            live = k < depth[...]
            return tuple(s + jnp.where(live, field_a[q, k], 0.0) for q, s in enumerate(sums))

        sums = levels_loop(c * span, (c + 1) * span, add, sums, 4)
    loads[1].wait()
    loads[2].wait()

    @pl.when(bottom)
    def _():
        pl.semaphore_wait(barrier, 4)

    @pl.when(jnp.logical_not(bottom))
    def _():
        pl.semaphore_wait(barrier, 5)

    pending = []
    stores = []
    for step in range(steps):
        moment = steps - 1 - step
        src, dst = (field_a, field_b) if step % 2 == 0 else (field_b, field_a)
        final = step == steps - 1
        if final:
            dst = out_h.at[0]
        scale = 1.0 / depth[...].astype(jnp.float32)
        for q in range(fields):
            share[step, q] = weight[q] * (scale * sums[q])
        couple = remote(step, COUPLE, share.at[step], flux.at[step], partner)
        couple.start()
        for copy in coeffs[moment]:
            copy.wait()

        for q in range(fields):
            north_out[step, q, 0:1] = jnp.zeros((1, cols), jnp.float32)
            south_out[step, q, 0:1] = jnp.zeros((1, cols), jnp.float32)

        def deep(k, packed):
            def put(q, up, down):
                north_out[step, q, pl.ds(k, 1)] = up
                south_out[step, q, pl.ds(k, 1)] = down

            return edges(
                step, moment, k, src, packed, lambda q: (q // half, (q % half) * levels + k), put
            )

        packed = levels_loop(1, levels, deep, (zero, zero), EDGE)
        for slot in range(2):
            col_out[step, slot] = packed[slot]
        send_e = remote(step, COL_E, col_out.at[step], col_w.at[step], east)
        send_w = remote(step, COL_W, col_out.at[step], col_e.at[step], west)
        send_rows = row_copies(step, ROW_N, ROW_S, north_out, south_out, north_in, south_in)
        start_rows(send_rows)
        send_e.start()
        send_w.start()

        couple.wait_recv()
        for q in range(fields):
            src[q, 0] = src[q, 0] + (flux[step, q] - share[step, q])

        def put_top(q, up, down):
            top_north_out[step, q:q + 1] = up
            top_south_out[step, q:q + 1] = down

        (top_packed,) = edges(step, moment, 0, src, (zero,), lambda q: (0, q), put_top)
        top_col_out[step] = top_packed
        top_e = remote(step, TOP_E, top_col_out.at[step], top_col_w.at[step], east)
        top_w = remote(step, TOP_W, top_col_out.at[step], top_col_e.at[step], west)
        top_rows = row_copies(
            step, TOP_N, TOP_S, top_north_out, top_south_out, top_north_in, top_south_in
        )
        start_rows(top_rows)
        top_e.start()
        top_w.start()

        def inner(k, carry):
            interior(moment, k, src, dst)
            return carry

        levels_loop(0, levels, inner, 0, INNER)

        for copy in (send_e, send_w, top_e, top_w):
            copy.wait_recv()
        for copies in (send_rows, top_rows):
            copies[1][0].wait_recv()
            pl.when(jnp.logical_not(bottom))(copies[0][0].wait_recv)

        @pl.when(top)
        def _():
            lane_s = lax.broadcasted_iota(jnp.int32, (levels, cols), 1)
            for q in range(fields):
                turned = reversed_lanes(north_in[step, q], lane_s)
                north_in[step, q] = turned if q < half else -turned
            lane_f = lax.broadcasted_iota(jnp.int32, (fields, cols), 1)
            sign = lax.broadcasted_iota(jnp.int32, (fields, cols), 0)
            turned = reversed_lanes(top_north_in[step], lane_f)
            top_north_in[step] = jnp.where(sign < half, turned, -turned)

        pair = [joined(col_w[step, slot], col_e[step, slot]) for slot in range(2)]
        top_pair = joined(top_col_w[step], top_col_e[step])
        sums = []
        for q in range(fields):
            total = finish(
                0, q, dst, top_pair, q,
                top_south_in[step, q:q + 1], top_north_in[step, q:q + 1],
            )
            sums.append(total)
        sums = tuple(sums)
        for c in range(chunk):

            def last(k, sums):
                out = []
                for q in range(fields):
                    total = finish(
                        k, q, dst, pair[q // half], (q % half) * levels + k,
                        south_in[step, q, pl.ds(k, 1)], north_in[step, q, pl.ds(k, 1)],
                    )
                    if not final:
                        out.append(sums[q] + jnp.where(k < depth[...], total, 0.0))
                return tuple(out) if not final else sums

            lower = max(1, c * span)
            sums = levels_loop(lower, (c + 1) * span, last, sums if not final else 0, LAST)

        pending += [(couple, None), (send_e, None), (send_w, None), (top_e, None), (top_w, None)]
        pending += send_rows + top_rows

    for copy, go in pending:
        if go is None:
            copy.wait_send()
        else:
            pl.when(go)(copy.wait_send)
    for copy in stores:
        copy.wait()


def solution(mesh):
    lats, lons = mesh.shape["lat"], mesh.shape["lon"]

    def shards(adjoint, land_mask, coupling_depth, coupling_weight, diffusion, velocity, mixing):
        _, fields, levels, rows, cols = adjoint.shape
        steps = diffusion.shape[0]
        chunk = 3
        f32 = jnp.float32
        block = (rows, cols)
        column = pltpu.VMEM((steps, 2, rows, cols), f32)
        top_column = pltpu.VMEM((steps, rows, cols), f32)
        edge = pltpu.VMEM((steps, fields, levels, cols), f32)
        top_edge = pltpu.VMEM((steps, fields, cols), f32)
        return pl.pallas_call(
            functools.partial(kernel, lats, lons),
            out_shape=jax.ShapeDtypeStruct(adjoint.shape, f32),
            in_specs=[pl.BlockSpec(memory_space=pltpu.HBM)] * 7,
            out_specs=pl.BlockSpec(memory_space=pltpu.VMEM),
            scratch_shapes=[
                pltpu.VMEM((fields, levels, rows, cols), f32),
                pltpu.VMEM((fields, levels, rows, cols), f32),
                pltpu.VMEM((steps, levels, rows, cols), f32),
                pltpu.VMEM((steps, 2, levels, rows, cols), f32),
                pltpu.VMEM((steps, levels, rows, cols), f32),
                pltpu.VMEM(block, jnp.int32),
                pltpu.VMEM(block, jnp.int32),
                pltpu.VMEM((fields, rows, cols), f32),
                pltpu.VMEM((fields, levels + 2, rows, cols), f32),
                pltpu.VMEM((steps, fields, rows, cols), f32),
                pltpu.VMEM((steps, fields, rows, cols), f32),
                column, column, column,
                top_column, top_column, top_column,
                edge, edge, edge, edge,
                top_edge, top_edge, top_edge, top_edge,
                pltpu.SemaphoreType.DMA((3 + chunk + 3 * steps,)),
                pltpu.SemaphoreType.DMA((chunk,)),
                pltpu.SemaphoreType.DMA((steps, 12)),
                pltpu.SemaphoreType.DMA((steps, 9)),
            ],
            compiler_params=pltpu.CompilerParams(
                collective_id=0, has_side_effects=True, vmem_limit_bytes=40 * 1024 * 1024
            ),
            name="adjoint",
        )(*(pltpu.with_memory_space_constraint(x, pltpu.HBM) for x in (adjoint, land_mask, coupling_depth, coupling_weight, diffusion, velocity, mixing)))

    in_specs = (
        P("ice", None, None, "lat", "lon"),
        P("lat", "lon"),
        P("ice", "lat", "lon"),
        P("ice", None, "lat", "lon"),
        P(None, "ice", None, "lat", "lon"),
        P(None, "ice", None, None, "lat", "lon"),
        P(None, "ice", None, "lat", "lon"),
    )
    out_specs = P("ice", None, None, "lat", "lon")
    return jax.shard_map(shards, mesh=mesh, in_specs=in_specs, out_specs=out_specs, check_vma=False)
```

```python
import functools

import jax
import jax.numpy as jnp
from jax import lax
from jax.experimental import pallas as pl
from jax.experimental.pallas import tpu as pltpu
from jax.sharding import PartitionSpec as P

MESH = pl.DeviceIdType.MESH
EDGE, INNER, LAST = 8, 4, 8
COUPLE, COL_E, COL_W, ROW_N, ROW_S, TOP_E, TOP_W, TOP_N, TOP_S = range(9)


def levels_loop(lower, upper, body, carry, times):
    whole = (upper - lower) // times

    def some(i, carry):
        for j in range(times):
            carry = body(lower + i * times + j, carry)
        return carry

    if whole > 0:
        carry = lax.fori_loop(0, whole, some, carry)
    for k in range(lower + whole * times, upper):
        carry = body(k, carry)
    return carry


def reversed_lanes(x, lane):
    width = x.shape[-1]
    bit = 1
    while bit < width:
        up = pltpu.roll(x, width - bit, x.ndim - 1)
        down = pltpu.roll(x, bit, x.ndim - 1)
        x = jnp.where((lane & bit) == 0, up, down)
        bit *= 2
    return x


def kernel(
    lats, lons, adj_h, mask_h, depth_h, weight_h, diff_h, vel_h, mix_h, out_h,
    field_a, field_b, diff, vel, mix, mask_i, depth, weight, vert,
    share, flux, col_out, col_w, col_e, top_col_out, top_col_w, top_col_e,
    north_out, south_out, north_in, south_in,
    top_north_out, top_south_out, top_north_in, top_south_in,
    load_sem, store_sem, send_sem, recv_sem,
):
    fields, levels, rows, cols = field_a.shape
    steps = diff.shape[0]
    chunk = store_sem.shape[0]
    span = levels // chunk
    ice, lat, lon = lax.axis_index("ice"), lax.axis_index("lat"), lax.axis_index("lon")
    partner = (1 - ice, lat, lon)
    east = (ice, lat, lax.rem(lon + 1, lons))
    west = (ice, lat, lax.rem(lon + lons - 1, lons))
    north = (ice, lat + 1, lon)
    south = (ice, lat - 1, lon)
    mirror = (ice, lat, lons - 1 - lon)
    top, bottom = lat == lats - 1, lat == 0

    loads = [
        pltpu.make_async_copy(depth_h.at[0], depth, load_sem.at[0]),
        pltpu.make_async_copy(weight_h.at[0], weight, load_sem.at[1]),
        pltpu.make_async_copy(mask_h, mask_i, load_sem.at[2]),
    ]
    for c in range(chunk):
        part = pl.ds(c * span, span)
        loads.append(pltpu.make_async_copy(adj_h.at[0, :, part], field_a.at[:, part], load_sem.at[3 + c]))
    coeffs = []
    for moment in range(steps):
        base = 3 + chunk + 3 * moment
        coeffs.append([
            pltpu.make_async_copy(diff_h.at[moment, 0], diff.at[moment], load_sem.at[base]),
            pltpu.make_async_copy(vel_h.at[moment, 0], vel.at[moment], load_sem.at[base + 1]),
            pltpu.make_async_copy(mix_h.at[moment, 0], mix.at[moment], load_sem.at[base + 2]),
        ])
    for copy in loads:
        copy.start()
    for moment in reversed(range(steps)):
        for copy in coeffs[moment]:
            copy.start()

    barrier = pltpu.get_barrier_semaphore()
    for peer in (partner, east, west):
        pl.semaphore_signal(barrier, inc=1, device_id=peer, device_id_type=MESH)

    @pl.when(top)
    def _():
        pl.semaphore_signal(barrier, inc=1, device_id=mirror, device_id_type=MESH)

    @pl.when(jnp.logical_not(top))
    def _():
        pl.semaphore_signal(barrier, inc=1, device_id=north, device_id_type=MESH)

    @pl.when(jnp.logical_not(bottom))
    def _():
        pl.semaphore_signal(barrier, inc=1, device_id=south, device_id_type=MESH)

    lane = lax.broadcasted_iota(jnp.int32, (rows, cols), 1)
    row = lax.broadcasted_iota(jnp.int32, (rows, cols), 0)
    lane8 = lax.broadcasted_iota(jnp.int32, (8, cols), 1)
    row8 = lax.broadcasted_iota(jnp.int32, (8, cols), 0)
    ends8 = jnp.logical_or(lane8 == 0, lane8 == cols - 1)
    for q in range(fields):
        vert[q, 0] = jnp.zeros((rows, cols), jnp.float32)
        vert[q, levels + 1] = jnp.zeros((rows, cols), jnp.float32)

    @pl.when(bottom)
    def _():
        south_in[...] = jnp.zeros_like(south_in)
        top_south_in[...] = jnp.zeros_like(top_south_in)

    def remote(step, which, src, dst, peer):
        return pltpu.make_async_remote_copy(
            src_ref=src, dst_ref=dst, send_sem=send_sem.at[step, which],
            recv_sem=recv_sem.at[step, which], device_id=peer, device_id_type=MESH,
        )

    def row_copies(step, which_n, which_s, n_out, s_out, n_in, s_in, part=()):
        at = (step,) + part
        return [
            (remote(step, which_s, n_out.at[at], s_in.at[at], north), jnp.logical_not(top)),
            (remote(step, which_n, n_out.at[at], n_in.at[at], mirror), top),
            (remote(step, which_n, s_out.at[at], n_in.at[at], south), jnp.logical_not(bottom)),
        ]

    def start_rows(copies):
        for copy, go in copies:
            pl.when(go)(copy.start)

    half = fields // 2

    def edges(step, moment, k, src, packed, place, put_rows):
        mask = mask_i[...].astype(jnp.float32)
        d, z = diff[moment, k] * mask, vel[moment, 0, k] * mask
        v = mix[moment, k] * mask
        both = d + jnp.where(lane == cols - 1, -z, z)
        last, first = slice(rows - 1, rows), slice(0, 1)
        b_last, b_first = vel[moment, 1, k, last] * mask[last], vel[moment, 1, k, first] * mask[first]
        to_north, to_south = d[last] - b_last, d[first] + b_first
        packed = list(packed)
        for q in range(fields):
            a = src[q, k]
            vert[q, k + 1] = v * a
            slot, spot = place(q)
            turned = pltpu.roll(both * a, 2 * spot + 1, 1)
            packed[slot] = jnp.where((lane >> 1) == spot, turned, packed[slot])
            put_rows(q, to_north * a[last], to_south * a[first])
        return tuple(packed)

    def interior(moment, k, src, dst):
        mask = mask_i[...].astype(jnp.float32)
        d, z, b = diff[moment, k] * mask, vel[moment, 0, k] * mask, vel[moment, 1, k] * mask
        own = mask - 4.0 * d - 2.0 * (mix[moment, k] * mask)
        eastward = jnp.where(lane == cols - 1, 0.0, d - z)
        westward = jnp.where(lane == 0, 0.0, d + z)
        northward = jnp.where(row == rows - 1, 0.0, d - b)
        southward = jnp.where(row == 0, 0.0, d + b)
        for q in range(fields):
            a = src[q, k]
            total = own * a + vert[q, k] + vert[q, k + 2]
            total = total + pltpu.roll(eastward * a, 1, 1) + pltpu.roll(westward * a, cols - 1, 1)
            total = total + pltpu.roll(northward * a, 1, 0) + pltpu.roll(southward * a, rows - 1, 0)
            dst[q, k] = total

    def finish(k, q, dst, packed, spot, from_south, from_north):
        parts = []
        for r in range(0, rows, 8):
            turned = pltpu.roll(packed[r:r + 8], cols - 1 - 2 * spot, 1)
            total = dst[q, k, r:r + 8] + jnp.where(ends8, turned, 0.0)
            if r == 0:
                total = total + jnp.where(row8 == 0, from_south, 0.0)
            if r == rows - 8:
                total = total + jnp.where(row8 == 7, from_north, 0.0)
            dst[q, k, r:r + 8] = total
            parts.append(total)
        return jnp.concatenate(parts, axis=0)

    def joined(from_west, from_east, turn_west, turn_east):
        if turn_west:
            from_west = pltpu.roll(from_west, turn_west, 1)
        if turn_east:
            from_east = pltpu.roll(from_east, turn_east, 1)
        return jnp.where((lane & 1) == 1, from_west, from_east)

    loads[0].wait()
    zero = jnp.zeros((rows, cols), jnp.float32)
    sums = (zero,) * fields
    for c in range(chunk):
        loads[3 + c].wait()

        def add(k, sums):
            live = k < depth[...]
            return tuple(s + jnp.where(live, field_a[q, k], 0.0) for q, s in enumerate(sums))

        sums = levels_loop(c * span, (c + 1) * span, add, sums, 4)
    loads[1].wait()
    loads[2].wait()

    @pl.when(bottom)
    def _():
        pl.semaphore_wait(barrier, 4)

    @pl.when(jnp.logical_not(bottom))
    def _():
        pl.semaphore_wait(barrier, 5)

    pending = []
    stores = []
    for step in range(steps):
        moment = steps - 1 - step
        src, dst = (field_a, field_b) if step % 2 == 0 else (field_b, field_a)
        final = step == steps - 1
        if final:
            dst = out_h.at[0]
        scale = 1.0 / depth[...].astype(jnp.float32)
        for q in range(fields):
            share[step, q] = weight[q] * (scale * sums[q])
        couple = remote(step, COUPLE, share.at[step], flux.at[step], partner)
        couple.start()
        for copy in coeffs[moment]:
            copy.wait()

        for q in range(fields):
            north_out[step, q, 0:1] = jnp.zeros((1, cols), jnp.float32)
            south_out[step, q, 0:1] = jnp.zeros((1, cols), jnp.float32)

        def deep(k, packed):
            def put(q, up, down):
                north_out[step, q, pl.ds(k, 1)] = up
                south_out[step, q, pl.ds(k, 1)] = down

            return edges(
                step, moment, k, src, packed, lambda q: (q // half, (q % half) * levels + k), put
            )

        packed = (zero, zero)
        groups = []
        for c in range(chunk):
            packed = levels_loop(max(1, c * span), (c + 1) * span, deep, packed, EDGE)
            part = pl.ds(c * span, span)
            which_n, which_s = (ROW_N, ROW_S) if c == 0 else (7 + 2 * c, 8 + 2 * c)
            groups.append(row_copies(
                step, which_n, which_s, north_out, south_out, north_in, south_in, (slice(None), part)
            ))
            start_rows(groups[-1])
        odd = (lane & 1) == 1
        col_out[step, 0] = jnp.where(odd, pltpu.roll(packed[1], 1, 1), packed[0])
        col_out[step, 1] = jnp.where(odd, packed[1], pltpu.roll(packed[0], cols - 1, 1))
        send_e = remote(step, COL_E, col_out.at[step, 0], col_w.at[step], east)
        send_w = remote(step, COL_W, col_out.at[step, 1], col_e.at[step], west)
        send_e.start()
        send_w.start()

        couple.wait_recv()
        for q in range(fields):
            src[q, 0] = src[q, 0] + (flux[step, q] - share[step, q])

        def put_top(q, up, down):
            top_north_out[step, q:q + 1] = up
            top_south_out[step, q:q + 1] = down

        (top_packed,) = edges(step, moment, 0, src, (zero,), lambda q: (0, q), put_top)
        top_col_out[step] = top_packed
        top_e = remote(step, TOP_E, top_col_out.at[step], top_col_w.at[step], east)
        top_w = remote(step, TOP_W, top_col_out.at[step], top_col_e.at[step], west)
        top_rows = row_copies(
            step, TOP_N, TOP_S, top_north_out, top_south_out, top_north_in, top_south_in
        )
        start_rows(top_rows)
        top_e.start()
        top_w.start()

        def inner(k, carry):
            interior(moment, k, src, dst)
            return carry

        levels_loop(0, levels, inner, 0, INNER)

        for copy in (send_e, send_w, top_e, top_w):
            copy.wait_recv()
        for copies in groups + [top_rows]:
            copies[1][0].wait_recv()
            pl.when(jnp.logical_not(bottom))(copies[0][0].wait_recv)

        @pl.when(top)
        def _():
            lane_s = lax.broadcasted_iota(jnp.int32, (levels, cols), 1)
            for q in range(fields):
                turned = reversed_lanes(north_in[step, q], lane_s)
                north_in[step, q] = turned if q < half else -turned
            lane_f = lax.broadcasted_iota(jnp.int32, (fields, cols), 1)
            sign = lax.broadcasted_iota(jnp.int32, (fields, cols), 0)
            turned = reversed_lanes(top_north_in[step], lane_f)
            top_north_in[step] = jnp.where(sign < half, turned, -turned)

        pair = [
            joined(col_w[step], col_e[step], 1, 0), joined(col_w[step], col_e[step], 0, cols - 1)
        ]
        top_pair = joined(top_col_w[step], top_col_e[step], 1, cols - 1)
        sums = []
        for q in range(fields):
            total = finish(
                0, q, dst, top_pair, q,
                top_south_in[step, q:q + 1], top_north_in[step, q:q + 1],
            )
            sums.append(total)
        sums = tuple(sums)
        for c in range(chunk):

            def last(k, sums):
                out = []
                for q in range(fields):
                    total = finish(
                        k, q, dst, pair[q // half], (q % half) * levels + k,
                        south_in[step, q, pl.ds(k, 1)], north_in[step, q, pl.ds(k, 1)],
                    )
                    if not final:
                        out.append(sums[q] + jnp.where(k < depth[...], total, 0.0))
                return tuple(out) if not final else sums

            lower = max(1, c * span)
            sums = levels_loop(lower, (c + 1) * span, last, sums if not final else 0, LAST)

        pending += [(couple, None), (send_e, None), (send_w, None), (top_e, None), (top_w, None)]
        for copies in groups + [top_rows]:
            pending += copies

    for copy, go in pending:
        if go is None:
            copy.wait_send()
        else:
            pl.when(go)(copy.wait_send)
    for copy in stores:
        copy.wait()


def solution(mesh):
    lats, lons = mesh.shape["lat"], mesh.shape["lon"]

    def shards(adjoint, land_mask, coupling_depth, coupling_weight, diffusion, velocity, mixing):
        _, fields, levels, rows, cols = adjoint.shape
        steps = diffusion.shape[0]
        chunk = 3
        f32 = jnp.float32
        block = (rows, cols)
        column = pltpu.VMEM((steps, 2, rows, cols), f32)
        top_column = pltpu.VMEM((steps, rows, cols), f32)
        edge = pltpu.VMEM((steps, fields, levels, cols), f32)
        top_edge = pltpu.VMEM((steps, fields, cols), f32)
        return pl.pallas_call(
            functools.partial(kernel, lats, lons),
            out_shape=jax.ShapeDtypeStruct(adjoint.shape, f32),
            in_specs=[pl.BlockSpec(memory_space=pltpu.HBM)] * 7,
            out_specs=pl.BlockSpec(memory_space=pltpu.VMEM),
            scratch_shapes=[
                pltpu.VMEM((fields, levels, rows, cols), f32),
                pltpu.VMEM((fields, levels, rows, cols), f32),
                pltpu.VMEM((steps, levels, rows, cols), f32),
                pltpu.VMEM((steps, 2, levels, rows, cols), f32),
                pltpu.VMEM((steps, levels, rows, cols), f32),
                pltpu.VMEM(block, jnp.int32),
                pltpu.VMEM(block, jnp.int32),
                pltpu.VMEM((fields, rows, cols), f32),
                pltpu.VMEM((fields, levels + 2, rows, cols), f32),
                pltpu.VMEM((steps, fields, rows, cols), f32),
                pltpu.VMEM((steps, fields, rows, cols), f32),
                column, top_column, top_column,
                top_column, top_column, top_column,
                edge, edge, edge, edge,
                top_edge, top_edge, top_edge, top_edge,
                pltpu.SemaphoreType.DMA((3 + chunk + 3 * steps,)),
                pltpu.SemaphoreType.DMA((chunk,)),
                pltpu.SemaphoreType.DMA((steps, 7 + 2 * chunk)),
                pltpu.SemaphoreType.DMA((steps, 7 + 2 * chunk)),
            ],
            compiler_params=pltpu.CompilerParams(
                collective_id=0, has_side_effects=True, vmem_limit_bytes=40 * 1024 * 1024
            ),
            name="adjoint",
        )(*(pltpu.with_memory_space_constraint(x, pltpu.HBM) for x in (adjoint, land_mask, coupling_depth, coupling_weight, diffusion, velocity, mixing)))

    in_specs = (
        P("ice", None, None, "lat", "lon"),
        P("lat", "lon"),
        P("ice", "lat", "lon"),
        P("ice", None, "lat", "lon"),
        P(None, "ice", None, "lat", "lon"),
        P(None, "ice", None, None, "lat", "lon"),
        P(None, "ice", None, "lat", "lon"),
    )
    out_specs = P("ice", None, None, "lat", "lon")
    return jax.shard_map(shards, mesh=mesh, in_specs=in_specs, out_specs=out_specs, check_vma=False)
```
